512 devices in a mesh: layer: 16 (over y, x), dp: 32 (over z, core).
Axes of the slice: x: 4, y: 4, z: 16, core: 2. Of those that a mesh axis runs over, the one named last changes fastest.
Arguments:
- inputs: bfloat16 [4096, 1024], P('dp'), may hold values from -6 to 6
- guess_fwd: float32 [16, 4096, 1024], P('layer', 'dp'), may hold values from -9 to 9
- guess_adj: float32 [16, 4096, 1024], P('layer', 'dp'), may hold values from -6 to 6
- weights: bfloat16 [32, 1024, 1024], P('layer', 'dp'), may hold values from -0.1875 to 0.1875
- biases: float32 [32, 1024], P('layer'), may hold values from -3 to 3
- gains: float32 [16, 1024], P('layer'), may hold values from 0.6 to 1
- cotangent: bfloat16 [4096, 1024], P('dp'), may hold values from -6 to 6
Outputs:
- block_ends: float32 [16, 4096, 1024], P('layer', 'dp')
- block_adjoints: float32 [16, 4096, 1024], P('layer', 'dp')
- weight_grad: float32 [32, 1024, 1024], P('layer', 'dp')
- coarse_ends: float32 [16, 4096, 1024], P('layer', 'dp')
- coarse_adjoints: float32 [16, 4096, 1024], P('layer', 'dp')
The draws below stay inside these ranges and needn't reach their ends.
All inputs are finite; a program needn't handle non-finite values.
Results may differ from the reference program's by a relative error of at most 0.024.
Values may be sent and summed in bfloat16 or wider, within the bound.
No kernel may reach another device: no remote copies, remote signals or barrier semaphores. Data moves between devices by JAX's collectives and lax.ppermute only.
A program may use at most 64 MiB of HBM per device.

```python
import jax
import jax.numpy as jnp
from jax import lax

D = 1024
ITERS = 1
ROWS_DEV = 128
BLOCKS = 16
LAYERS = 32
ROWS = 4096
N_DP = 32


def shard_levels(key, shape, split, smallest, top_value):
    gain = 1.0
    for axis_at, blocks in split:
        steps = jax.random.uniform(jax.random.fold_in(jax.random.fold_in(key, 6), axis_at), (blocks,), jnp.float32, smallest / len(split), top_value / len(split))
        gain = gain * jnp.repeat(jnp.exp(steps), shape[axis_at] // blocks).reshape((-1,) + (1,) * (len(shape) - 1 - axis_at))
    return gain


def normal_values(own_key, shape, spread, bound, cuts=(), dtype=jnp.bfloat16):
    values = jax.random.normal(own_key, shape, jnp.float32) * spread
    if len(cuts) > 0:
        values = shard_levels(own_key, shape, cuts, -0.22, 0.18) * values
    return jnp.clip(values, min=-bound, max=bound).astype(dtype)


def setup_inputs(seed: int = 0) -> dict:
    streams_of = jax.random.split(jax.random.key(seed), 8)
    return {
        "inputs": normal_values(streams_of[0], (ROWS, D), 1.0, 6.0, ((0, 32),)),
        "guess_fwd": normal_values(streams_of[1], (BLOCKS, ROWS, D), 1.5, 9.0, ((0, 16), (1, 32)), jnp.float32),
        "guess_adj": normal_values(streams_of[2], (BLOCKS, ROWS, D), 1.0, 6.0, ((0, 16), (1, 32)), jnp.float32),
        "weights": normal_values(streams_of[3], (LAYERS, D, D), D ** -0.5, 0.1875, ((0, 16), (1, 32))),
        "biases": normal_values(streams_of[4], (LAYERS, D), 0.5, 3.0, ((0, 16),), jnp.float32),
        "gains": jnp.clip(0.6 + 0.39999998 * jax.random.uniform(streams_of[5], (BLOCKS, D), jnp.float32) ** shard_levels(streams_of[5], (BLOCKS, D), ((0, 16),), -0.2, 0.2), 0.6, 1.0),
        "cotangent": normal_values(streams_of[6], (ROWS, D), 1.0, 6.0, ((0, 32),)),
    }


step_size = 0.5


def forward_block(start, weights, biases):
    state = start
    kept = []
    slopes = []
    for j in range(weights.shape[0]):
        rounded = state.astype(jnp.bfloat16)
        active = jnp.tanh(jnp.dot(rounded, weights[j], preferred_element_type=jnp.float32) + biases[j])
        kept.append(rounded)
        slopes.append(1.0 - active * active)
        state = state + step_size * active
    return state, kept, slopes


def backward_block(end, weights, slopes):
    adjoint = end
    pieces = [None] * weights.shape[0]
    for j in reversed(range(weights.shape[0])):
        scaled = (adjoint * slopes[j]).astype(jnp.bfloat16)
        pieces[j] = scaled
        adjoint = adjoint + step_size * jnp.dot(scaled, weights[j].T, preferred_element_type=jnp.float32)
    return adjoint, pieces


def reference(inputs, guess_fwd, guess_adj, weights, biases, gains, cotangent):
    blocks = guess_fwd.shape[0]
    per = weights.shape[0] // blocks
    anchor = inputs.astype(jnp.float32)
    guess = [guess_fwd[k] for k in range(blocks)]
    starts = [anchor] + guess[:-1]
    for turn in range(ITERS):
        ends = [forward_block(starts[k], weights[k * per:(k + 1) * per], biases[k * per:(k + 1) * per])[0] for k in range(blocks)]
        carry = jnp.zeros_like(anchor)
        fresh = []
        for k in range(blocks):
            carry = gains[k] * carry + (ends[k] - guess[k])
            fresh.append(guess[k] + carry)
        guess = fresh
        starts = [anchor] + guess[:-1]
    finals = [forward_block(starts[k], weights[k * per:(k + 1) * per], biases[k * per:(k + 1) * per]) for k in range(blocks)]
    block_ends = jnp.stack([item[0] for item in finals])
    final_adj = cotangent.astype(jnp.float32)
    lam = [guess_adj[k] for k in range(blocks)]
    ends_adj = lam[1:] + [final_adj]
    for turn in range(ITERS):
        backs = [backward_block(ends_adj[k], weights[k * per:(k + 1) * per], finals[k][2])[0] for k in range(blocks)]
        carry = jnp.zeros_like(final_adj)
        fresh = [None] * blocks
        for k in reversed(range(blocks)):
            carry = gains[k] * carry + (backs[k] - lam[k])
            fresh[k] = lam[k] + carry
        lam = fresh
        ends_adj = lam[1:] + [final_adj]
    adjoints = []
    grads = []
    for k in range(blocks):
        adjoint, pieces = backward_block(ends_adj[k], weights[k * per:(k + 1) * per], finals[k][2])
        adjoints.append(adjoint)
        for j in range(per):
            left = finals[k][1][j].astype(jnp.float32).reshape(N_DP, ROWS_DEV, D)
            right = pieces[j].astype(jnp.float32).reshape(N_DP, ROWS_DEV, D)
            parts = step_size * jnp.einsum("prd,pre->pde", left, right, precision=lax.Precision.HIGHEST)
            parts = lax.optimization_barrier(parts.astype(jnp.bfloat16))
            grads.append(jnp.sum(parts.astype(jnp.float32), axis=0))
    return block_ends, jnp.stack(adjoints), jnp.stack(grads), jnp.stack(guess), jnp.stack(lam)
```

```python
import functools

import jax
import jax.numpy as jnp
from jax import lax
from jax.experimental import pallas as pl
from jax.experimental.pallas import tpu as pltpu
from jax.sharding import Mesh, PartitionSpec as P

step_size = 0.5
bf16 = jnp.bfloat16
f32 = jnp.float32


def from_behind(block, axis, distance):
    devices = range(lax.axis_size(axis))
    route = [(i - distance, i) for i in devices if i - distance in devices]
    return lax.ppermute(block, axis, route)


def scan_kernel(ends_ref, guess_ref, gains_ref, edge_ref, starts_ref, *, first, reverse):
    blocks, rows = ends_ref.shape[:2]
    carry = jnp.zeros(ends_ref.shape[1:], f32)
    order = range(blocks - 1, -1, -1) if reverse else range(blocks)
    step = -1 if reverse else 1
    starts_ref[order[0]] = edge_ref[...]
    for k in order[:-1]:
        guess = guess_ref[k, first : first + rows, :]
        resid = ends_ref[k].astype(f32) - guess
        carry = gains_ref[k : k + 1, :] * carry + resid
        starts_ref[k + step] = (guess + carry).astype(starts_ref.dtype)


def corrected(end, guess_rows, gains_all, edge_rows, reverse):
    blocks = lax.axis_size("layer")
    rows, width = end.shape
    pieces = end.reshape(blocks, rows // blocks, width)
    mine = lax.all_to_all(pieces, "layer", 0, 0)
    starts = pl.pallas_call(
        functools.partial(
            scan_kernel, first=rows // blocks if reverse else 0, reverse=reverse
        ),
        out_shape=jax.ShapeDtypeStruct(mine.shape, bf16),
        name="coarse_scan",
    )(mine, guess_rows, gains_all, edge_rows)
    return lax.all_to_all(starts, "layer", 0, 0).reshape(rows, width)


def fetch(weights_hbm, held, sems, layers):
    bands = sems.shape[1]
    size = held.shape[1] // bands
    copies = {}
    for l in layers:
        for n in range(bands):
            band = pl.ds(n * size, size)
            copies[l, n] = pltpu.make_async_copy(
                weights_hbm.at[l, band, :], held.at[l, band, :], sems.at[l, n]
            )
            copies[l, n].start()
    return copies


def forward_layer(rounded, l, held, biases_ref, copies, bands):
    size = held.shape[1] // bands
    total = biases_ref[l : l + 1, :]
    for n in range(bands):
        if (l, n) in copies:
            copies[l, n].wait()
        band = slice(n * size, (n + 1) * size)
        total = total + jnp.dot(
            rounded[:, band], held[l, band, :], preferred_element_type=f32
        )
    return jnp.tanh(total)


def back_step(scaled, weight):
    return step_size * lax.dot_general(
        scaled, weight, (((1,), (1,)), ((), ())), preferred_element_type=f32
    )


def relax_kernel(start_ref, w_ref, b_ref, end_ref, rounded_ref, held, sems):
    layers, bands = sems.shape
    copies = fetch(w_ref, held, sems, range(layers))
    state = start_ref[...]
    for l in range(layers):
        active = forward_layer(state.astype(bf16), l, held, b_ref, copies, bands)
        state = state + step_size * active
    end_ref[...] = state
    rounded_ref[...] = state.astype(bf16)


def both_ways_kernel(
    start_ref, w_ref, b_ref, adj_ref,
    end_ref, kept_ref, slopes_ref, back_ref, rounded_ref, held, sems,
):
    layers, bands = sems.shape
    copies = fetch(w_ref, held, sems, range(layers))
    state = start_ref[...].astype(f32)
    for l in range(layers):
        rounded = state.astype(bf16)
        kept_ref[l] = rounded
        active = forward_layer(rounded, l, held, b_ref, copies, bands)
        slopes_ref[l] = 1.0 - active * active
        state = state + step_size * active
    end_ref[...] = state
    adjoint = adj_ref[...]
    for l in reversed(range(layers)):
        scaled = (adjoint * slopes_ref[l]).astype(bf16)
        adjoint = adjoint + back_step(scaled, held[l])
    back_ref[...] = adjoint
    rounded_ref[...] = adjoint.astype(bf16)


def grads_kernel(
    core_ref, adj_ref, slopes_ref, kept_ref, w_ref,
    mine_ref, theirs_ref, adj_out_ref, scaled_ref, held, sems,
):
    layers, bands = sems.shape
    chips, _, rows, width = mine_ref.shape
    copies = fetch(w_ref, held, sems, range(1, layers))
    first = core_ref[0] == 0
    parts = 4
    adjoint = adj_ref[...].astype(f32)
    for l in reversed(range(layers)):
        scaled = (adjoint * slopes_ref[l]).astype(bf16)
        size = width // parts
        for m in range(parts):
            grad = step_size * lax.dot_general(
                kept_ref[l, :, m * size : (m + 1) * size],
                scaled,
                (((0,), (0,)), ((), ())),
                preferred_element_type=f32,
            )
            grad = grad.reshape(chips // parts, 2, rows, width)
            at = slice(m * chips // parts, (m + 1) * chips // parts)
            zero, one = grad[:, 0], grad[:, 1]
            mine_ref[at, l] = jnp.where(first, zero, one).astype(bf16)
            theirs_ref[at, l] = jnp.where(first, one, zero).astype(bf16)
        if l:
            for n in range(bands):
                copies[l, n].wait()
            adjoint = adjoint + back_step(scaled, held[l])
        else:
            adj_out_ref[...] = adjoint
            scaled_ref[...] = scaled


def call(kernel, name, outs, weights, ins, bands=4, smem=0):
    vmem = pl.BlockSpec(memory_space=pltpu.VMEM)
    specs = [pl.BlockSpec(memory_space=pltpu.SMEM)] * smem
    specs += [vmem] * (len(ins) - smem)
    at = [i for i, x in enumerate(ins) if x is weights][0]
    specs[at] = pl.BlockSpec(memory_space=pl.ANY)
    return pl.pallas_call(
        kernel,
        in_specs=specs,
        out_specs=[vmem] * len(outs),
        out_shape=[jax.ShapeDtypeStruct(*o) for o in outs],
        scratch_shapes=[
            pltpu.VMEM(weights.shape, weights.dtype),
            pltpu.SemaphoreType.DMA((weights.shape[0], bands)),
        ],
        name=name,
    )(*ins)


def local(inputs, guess_fwd, guess_adj, weights, biases, gains, cotangent):
    full_weights = lax.all_gather(weights, ("z", "c"), axis=1, tiled=True)
    layers, _, width = full_weights.shape
    count = lax.axis_size("layer")
    index = lax.axis_index("layer")
    rows = inputs.shape[0]
    own = rows // count
    guess = guess_fwd[0]
    lam = guess_adj[0]
    arrived = from_behind(guess, "layer", 1)
    arrived_adj = from_behind(lam, "layer", -1)
    gains_all = lax.all_to_all(
        jnp.broadcast_to(gains[None], (count, 1, width)), "layer", 0, 0
    ).reshape(count, width)
    guess_rows = lax.all_to_all(
        jnp.concatenate(
            [guess.reshape(count, own, width), lam.reshape(count, own, width)], 1
        ),
        "layer",
        0,
        0,
    )
    anchor_rows = lax.dynamic_slice_in_dim(inputs, own * index, own)
    final_rows = lax.dynamic_slice_in_dim(cotangent, own * index, own)
    guess_start = jnp.where(index == 0, inputs.astype(f32), arrived)
    guess_end = jnp.where(index == count - 1, cotangent.astype(f32), arrived_adj)
    guess_start, guess_end, gains_all, guess_rows, anchor_rows, final_rows = (
        lax.optimization_barrier(
            (guess_start, guess_end, gains_all, guess_rows, anchor_rows, final_rows)
        )
    )
    tall = (rows, width)
    relaxed, relaxed_low = call(
        relax_kernel, "relax", [(tall, f32), (tall, bf16)], full_weights,
        (guess_start, full_weights, biases),
    )
    start = corrected(relaxed_low, guess_rows, gains_all, anchor_rows, False)
    every = (layers, rows, width)
    end_state, kept, slopes, back, back_low = call(
        both_ways_kernel, "both_ways",
        [(tall, f32), (every, bf16), (every, f32), (tall, f32), (tall, bf16)],
        full_weights, (start, full_weights, biases, guess_end),
    )
    end_adj = corrected(back_low, guess_rows, gains_all, final_rows, True)
    core = lax.axis_index("c").astype(jnp.int32).reshape(1)
    chips, cores = lax.axis_size("z"), lax.axis_size("c")
    half = ((chips, layers, width // (chips * cores), width), bf16)
    mine, theirs, adjoint, scaled = call(
        grads_kernel, "grads", [half, half, (tall, f32), (tall, bf16)],
        full_weights, (core, end_adj, slopes, kept, full_weights), smem=1,
    )
    theirs = lax.ppermute(theirs, "c", [(0, 1), (1, 0)])
    total = lax.psum_scatter(mine + theirs, "z", scatter_dimension=0, tiled=True)
    adjoint = adjoint + back_step(scaled, full_weights[0])
    coarse = relaxed + gains * (start.astype(f32) - guess_start)
    coarse_adj = back + gains * (end_adj.astype(f32) - guess_end)
    return (
        end_state[None],
        adjoint[None],
        total[0].astype(f32),
        coarse[None],
        coarse_adj[None],
    )


def solution(mesh):
    layers, dp = mesh.devices.shape
    split = Mesh(mesh.devices.reshape(layers, dp // 2, 2), ("layer", "z", "c"))
    rows = ("z", "c")
    return jax.shard_map(
        local,
        mesh=split,
        in_specs=(
            P(rows, None),
            P("layer", rows, None),
            P("layer", rows, None),
            P("layer", rows, None),
            P("layer", None),
            P("layer", None),
            P(rows, None),
        ),
        out_specs=(
            P("layer", rows, None),
            P("layer", rows, None),
            P("layer", rows, None),
            P("layer", rows, None),
            P("layer", rows, None),
        ),
        check_vma=False,
    )
```

```python
import functools

import jax
import jax.numpy as jnp
from jax import lax
from jax.experimental import pallas as pl
from jax.experimental.pallas import tpu as pltpu
from jax.sharding import Mesh, PartitionSpec as P

step_size = 0.5
bf16 = jnp.bfloat16
f32 = jnp.float32
VMEM = pl.BlockSpec(memory_space=pltpu.VMEM)
SMALL = pltpu.CompilerParams(vmem_limit_bytes=20 * 2**20)


def from_behind(block, axis, distance):
    devices = range(lax.axis_size(axis))
    route = [(i - distance, i) for i in devices if i - distance in devices]
    return lax.ppermute(block, axis, route)


def scan_kernel(ends_ref, guess_ref, gains_ref, edge_ref, starts_ref, *, first, reverse):
    blocks, rows = ends_ref.shape[:2]
    carry = jnp.zeros(ends_ref.shape[1:], f32)
    order = range(blocks - 1, -1, -1) if reverse else range(blocks)
    step = -1 if reverse else 1
    starts_ref[order[0]] = edge_ref[...]
    for k in order[:-1]:
        guess = guess_ref[k, first : first + rows, :]
        resid = ends_ref[k].astype(f32) - guess
        carry = gains_ref[k : k + 1, :] * carry + resid
        starts_ref[k + step] = (guess + carry).astype(starts_ref.dtype)


def corrected(end, guess_rows, gains_all, edge_rows, reverse):
    blocks = lax.axis_size("layer")
    rows, width = end.shape
    pieces = end.reshape(blocks, rows // blocks, width)
    mine = lax.all_to_all(pieces, "layer", 0, 0)
    starts = pl.pallas_call(
        functools.partial(
            scan_kernel, first=rows // blocks if reverse else 0, reverse=reverse
        ),
        in_specs=[VMEM] * 4,
        out_specs=VMEM,
        out_shape=pltpu.VMEM(mine.shape, bf16),
        compiler_params=SMALL,
        name="coarse_scan",
    )(*map(near, (mine, guess_rows, gains_all, edge_rows)))
    return lax.all_to_all(starts, "layer", 0, 0).reshape(rows, width)


def fetch(weights_hbm, held, sems, layers):
    bands = sems.shape[1]
    size = held.shape[1] // bands
    copies = {}
    for l in layers:
        for n in range(bands):
            band = pl.ds(n * size, size)
            copies[l, n] = pltpu.make_async_copy(
                weights_hbm.at[band, l], held.at[l, band], sems.at[l, n]
            )
            copies[l, n].start()
    return copies


def forward_layer(rounded, l, held, biases_ref, copies, bands):
    size = held.shape[1] // bands
    width = held.shape[3]
    total = biases_ref[l : l + 1, :]
    for n in range(bands):
        copies[l, n].wait()
        weight = held[l, n * size : (n + 1) * size].reshape(-1, width)
        tall = weight.shape[0]
        total = total + jnp.dot(
            rounded[:, n * tall : (n + 1) * tall], weight, preferred_element_type=f32
        )
    return jnp.tanh(total)


def square(weight):
    return weight.reshape(-1, weight.shape[-1])


def back_step(scaled, weight):
    return step_size * lax.dot_general(
        scaled, weight, (((1,), (1,)), ((), ())), preferred_element_type=f32
    )


def relax_kernel(w_ref, start_ref, b_ref, end_ref, rounded_ref, held, sems):
    layers, bands = sems.shape
    copies = fetch(w_ref, held, sems, range(layers))
    state = start_ref[...]
    for l in range(layers):
        active = forward_layer(state.astype(bf16), l, held, b_ref, copies, bands)
        state = state + step_size * active
    end_ref[...] = state
    rounded_ref[...] = state.astype(bf16)


def both_ways_kernel(
    w_ref, start_ref, b_ref, adj_ref,
    end_ref, kept_ref, slopes_ref, back_ref, rounded_ref, held, sems,
):
    layers, bands = sems.shape
    copies = fetch(w_ref, held, sems, range(layers))
    state = start_ref[...].astype(f32)
    for l in range(layers):
        rounded = state.astype(bf16)
        if l:
            kept_ref[l - 1] = rounded
        active = forward_layer(rounded, l, held, b_ref, copies, bands)
        slopes_ref[l] = 1.0 - active * active
        state = state + step_size * active
    end_ref[...] = state
    adjoint = adj_ref[...]
    for l in reversed(range(layers)):
        scaled = (adjoint * slopes_ref[l]).astype(bf16)
        adjoint = adjoint + back_step(scaled, square(held[l]))
    back_ref[...] = adjoint
    rounded_ref[...] = adjoint.astype(bf16)


def grads_kernel(
    core_ref, w_ref, adj_ref, slopes_ref, start_ref, kept_ref,
    mine_ref, theirs_ref, adj_out_ref, scaled_ref, held, sems,
):
    layers, bands = sems.shape
    chips, _, rows, width = mine_ref.shape
    copies = fetch(w_ref, held, sems, range(1, layers))
    first = core_ref[0] == 0
    parts = 4
    adjoint = adj_ref[...].astype(f32)
    for l in reversed(range(layers)):
        scaled = (adjoint * slopes_ref[l]).astype(bf16)
        size = width // parts
        for m in range(parts):
            columns = slice(m * size, (m + 1) * size)
            kept = kept_ref[l - 1, :, columns] if l else start_ref[:, columns]
            grad = step_size * lax.dot_general(
                kept,
                scaled,
                (((0,), (0,)), ((), ())),
                preferred_element_type=f32,
            )
            grad = grad.reshape(chips // parts, 2, rows, width)
            at = slice(m * chips // parts, (m + 1) * chips // parts)
            zero, one = grad[:, 0], grad[:, 1]
            mine_ref[at, l] = jnp.where(first, zero, one).astype(bf16)
            theirs_ref[at, l] = jnp.where(first, one, zero).astype(bf16)
        if l:
            for n in range(bands):
                copies[l, n].wait()
            adjoint = adjoint + back_step(scaled, square(held[l]))
        else:
            adj_out_ref[...] = adjoint
            scaled_ref[...] = scaled


def add_kernel(mine_ref, theirs_ref, both_ref, sums, sems):
    copies = []
    parts = sems.shape[0]
    size = sums.shape[0] // parts
    for n in range(parts):
        part = pl.ds(n * size, size)
        sums[part] = mine_ref[part] + theirs_ref[part]
        copies.append(
            pltpu.make_async_copy(sums.at[part], both_ref.at[part], sems.at[n])
        )
        copies[n].start()
    for copy in copies:
        copy.wait()


def near(x):
    return pltpu.with_memory_space_constraint(x, pltpu.VMEM)


FAR, NEAR = pltpu.HBM, pltpu.VMEM


def call(kernel, name, outs, weights, ins, bands=4, scalars=()):
    count, layers, rows, width = weights.shape
    return pl.pallas_call(
        kernel,
        in_specs=[pl.BlockSpec(memory_space=pltpu.SMEM)] * len(scalars)
        + [pl.BlockSpec(memory_space=pl.ANY)]
        + [VMEM] * len(ins),
        out_specs=[VMEM] * len(outs),
        out_shape=outs,
        scratch_shapes=[
            pltpu.VMEM((layers, count, rows, width), weights.dtype),
            pltpu.SemaphoreType.DMA((layers, bands)),
        ],
        compiler_params=SMALL,
        name=name,
    )(*scalars, pltpu.with_memory_space_constraint(weights, pltpu.HBM), *map(near, ins))


def local(inputs, guess_fwd, guess_adj, weights, biases, gains, cotangent):
    full_weights = lax.all_gather(weights, ("z", "c"))
    _, layers, _, width = full_weights.shape
    count = lax.axis_size("layer")
    index = lax.axis_index("layer")
    rows = inputs.shape[0]
    own = rows // count
    guess = guess_fwd[0]
    lam = guess_adj[0]
    arrived = from_behind(guess, "layer", 1)
    arrived_adj = from_behind(lam, "layer", -1)
    gains_all = lax.all_to_all(
        jnp.broadcast_to(gains[None], (count, 1, width)), "layer", 0, 0
    ).reshape(count, width)
    guess_rows = lax.all_to_all(
        jnp.concatenate(
            [guess.reshape(count, own, width), lam.reshape(count, own, width)], 1
        ),
        "layer",
        0,
        0,
    )
    anchor_rows = lax.dynamic_slice_in_dim(inputs, own * index, own)
    final_rows = lax.dynamic_slice_in_dim(cotangent, own * index, own)
    guess_start = jnp.where(index == 0, inputs.astype(f32), arrived)
    guess_end = jnp.where(index == count - 1, cotangent.astype(f32), arrived_adj)
    guess_start, guess_end, gains_all, guess_rows, anchor_rows, final_rows = (
        lax.optimization_barrier(
            (guess_start, guess_end, gains_all, guess_rows, anchor_rows, final_rows)
        )
    )
    tall = (rows, width)
    relaxed, relaxed_low = call(
        relax_kernel, "relax", [FAR(tall, f32), NEAR(tall, bf16)],
        full_weights, (guess_start, biases),
    )
    start = corrected(relaxed_low, guess_rows, gains_all, anchor_rows, False)
    every, later = (layers, rows, width), (layers - 1, rows, width)
    end_state, kept, slopes, back, back_low = call(
        both_ways_kernel, "both_ways",
        [FAR(tall, f32), NEAR(later, bf16), NEAR(every, f32), FAR(tall, f32), NEAR(tall, bf16)],
        full_weights, (start, biases, guess_end),
    )
    end_adj = corrected(back_low, guess_rows, gains_all, final_rows, True)
    core = lax.axis_index("c").astype(jnp.int32).reshape(1)
    chips, cores = lax.axis_size("z"), lax.axis_size("c")
    half = (chips, layers, width // (chips * cores), width)
    mine, theirs, adjoint, scaled = call(
        grads_kernel, "grads",
        [NEAR(half, bf16), NEAR(half, bf16), FAR(tall, f32), FAR(tall, bf16)],
        full_weights, (end_adj, slopes, start, kept), scalars=(core,),
    )
    theirs = lax.ppermute(theirs, "c", [(0, 1), (1, 0)])
    both = pl.pallas_call(
        add_kernel,
        in_specs=[VMEM] * 2,
        out_specs=pl.BlockSpec(memory_space=pl.ANY),
        out_shape=jax.ShapeDtypeStruct(half, bf16),
        scratch_shapes=[pltpu.VMEM(half, bf16), pltpu.SemaphoreType.DMA((4,))],
        compiler_params=SMALL,
        name="add_halves",
    )(near(mine), near(theirs))
    total = lax.psum_scatter(both, "z", scatter_dimension=0, tiled=True)
    adjoint = adjoint + back_step(scaled, square(full_weights[:, 0]))
    coarse = relaxed + gains * (start.astype(f32) - guess_start)
    coarse_adj = back + gains * (end_adj.astype(f32) - guess_end)
    return (
        end_state[None],
        adjoint[None],
        total[0].astype(f32),
        coarse[None],
        coarse_adj[None],
    )


def solution(mesh):
    layers, dp = mesh.devices.shape
    split = Mesh(mesh.devices.reshape(layers, dp // 2, 2), ("layer", "z", "c"))
    rows = ("z", "c")
    return jax.shard_map(
        local,
        mesh=split,
        in_specs=(
            P(rows, None),
            P("layer", rows, None),
            P("layer", rows, None),
            P("layer", rows, None),
            P("layer", None),
            P("layer", None),
            P(rows, None),
        ),
        out_specs=(
            P("layer", rows, None),
            P("layer", rows, None),
            P("layer", rows, None),
            P("layer", rows, None),
            P("layer", rows, None),
        ),
        check_vma=False,
    )
```

```python
import functools

import jax
import jax.numpy as jnp
from jax import lax
from jax.experimental import pallas as pl
from jax.experimental.pallas import tpu as pltpu
from jax.sharding import Mesh, PartitionSpec as P

step_size = 0.5
bf16 = jnp.bfloat16
f32 = jnp.float32
VMEM = pl.BlockSpec(memory_space=pltpu.VMEM)
SMALL = pltpu.CompilerParams(vmem_limit_bytes=20 * 2**20)


def from_behind(block, axis, distance):
    devices = range(lax.axis_size(axis))
    route = [(i - distance, i) for i in devices if i - distance in devices]
    return lax.ppermute(block, axis, route)


def scan_kernel(ends_ref, guess_ref, gains_ref, edge_ref, starts_ref, *, reverse):
    blocks = ends_ref.shape[0]
    carry = jnp.zeros(ends_ref.shape[1:], f32)
    order = range(blocks - 1, -1, -1) if reverse else range(blocks)
    step = -1 if reverse else 1
    starts_ref[order[0]] = edge_ref[...]
    for k in order[:-1]:
        guess = guess_ref[k]
        resid = ends_ref[k].astype(f32) - guess
        carry = gains_ref[k : k + 1, :] * carry + resid
        starts_ref[k + step] = (guess + carry).astype(starts_ref.dtype)


def corrected(end, guess_rows, gains_all, edge_rows, reverse):
    blocks = lax.axis_size("layer")
    rows, width = end.shape
    pieces = end.reshape(blocks, rows // blocks, width)
    mine = lax.all_to_all(pieces, "layer", 0, 0)
    starts = pl.pallas_call(
        functools.partial(scan_kernel, reverse=reverse),
        in_specs=[VMEM] * 4,
        out_specs=VMEM,
        out_shape=pltpu.VMEM(mine.shape, bf16),
        compiler_params=SMALL,
        name="coarse_scan",
    )(*map(near, (mine, guess_rows, gains_all, edge_rows)))
    return lax.all_to_all(starts, "layer", 0, 0).reshape(rows, width)


def fetch(weights_hbm, held, sems, layers):
    bands = sems.shape[1]
    size = held.shape[1] // bands
    copies = {}
    for l in layers:
        for n in range(bands):
            band = pl.ds(n * size, size)
            copies[l, n] = pltpu.make_async_copy(
                weights_hbm.at[band, l], held.at[l, band], sems.at[l, n]
            )
            copies[l, n].start()
    return copies


def forward_layer(rounded, l, held, biases_ref, copies, bands):
    size = held.shape[1] // bands
    width = held.shape[3]
    total = biases_ref[l : l + 1, :]
    for n in range(bands):
        copies[l, n].wait()
        weight = held[l, n * size : (n + 1) * size].reshape(-1, width)
        tall = weight.shape[0]
        total = total + jnp.dot(
            rounded[:, n * tall : (n + 1) * tall], weight, preferred_element_type=f32
        )
    return jnp.tanh(total)


def square(weight):
    return weight.reshape(-1, weight.shape[-1])


def back_step(scaled, weight):
    return step_size * lax.dot_general(
        scaled, weight, (((1,), (1,)), ((), ())), preferred_element_type=f32
    )


def relax_kernel(w_ref, start_ref, b_ref, end_ref, rounded_ref, held, sems):
    layers, bands = sems.shape
    copies = fetch(w_ref, held, sems, range(layers))
    state = start_ref[...]
    for l in range(layers):
        active = forward_layer(state.astype(bf16), l, held, b_ref, copies, bands)
        state = state + step_size * active
    end_ref[...] = state
    rounded_ref[...] = state.astype(bf16)


def both_ways_kernel(
    w_ref, start_ref, b_ref, adj_ref,
    end_ref, kept_ref, slopes_ref, back_ref, rounded_ref, held, sems,
):
    layers, bands = sems.shape
    copies = fetch(w_ref, held, sems, range(layers))
    state = start_ref[...].astype(f32)
    for l in range(layers):
        rounded = state.astype(bf16)
        if l:
            kept_ref[l - 1] = rounded
        active = forward_layer(rounded, l, held, b_ref, copies, bands)
        slopes_ref[l] = 1.0 - active * active
        state = state + step_size * active
    end_ref[...] = state
    adjoint = adj_ref[...]
    for l in reversed(range(layers)):
        scaled = (adjoint * slopes_ref[l]).astype(bf16)
        adjoint = adjoint + back_step(scaled, square(held[l]))
    back_ref[...] = adjoint
    rounded_ref[...] = adjoint.astype(bf16)


def grads_kernel(
    core_ref, w_ref, adj_ref, slopes_ref, start_ref, kept_ref,
    mine_ref, theirs_ref, adj_out_ref, scaled_ref, held, sems,
):
    layers, bands = sems.shape
    chips, _, rows, width = mine_ref.shape
    copies = fetch(w_ref, held, sems, range(1, layers))
    first = core_ref[0] == 0
    parts = 4
    adjoint = adj_ref[...].astype(f32)
    for l in reversed(range(layers)):
        scaled = (adjoint * slopes_ref[l]).astype(bf16)
        size = width // parts
        for m in range(parts):
            columns = slice(m * size, (m + 1) * size)
            kept = kept_ref[l - 1, :, columns] if l else start_ref[:, columns]
            grad = step_size * lax.dot_general(
                kept,
                scaled,
                (((0,), (0,)), ((), ())),
                preferred_element_type=f32,
            )
            grad = grad.reshape(chips // parts, 2, rows, width)
            at = slice(m * chips // parts, (m + 1) * chips // parts)
            zero, one = grad[:, 0], grad[:, 1]
            mine_ref[at, l] = jnp.where(first, zero, one).astype(bf16)
            theirs_ref[at, l] = jnp.where(first, one, zero).astype(bf16)
        if l:
            for n in range(bands):
                copies[l, n].wait()
            adjoint = adjoint + back_step(scaled, square(held[l]))
        else:
            adj_out_ref[...] = adjoint
            scaled_ref[...] = scaled


def add_kernel(mine_ref, theirs_ref, both_ref, sums, sems):
    copies = []
    parts = sems.shape[0]
    size = sums.shape[0] // parts
    for n in range(parts):
        part = pl.ds(n * size, size)
        sums[part] = mine_ref[part] + theirs_ref[part]
        copies.append(
            pltpu.make_async_copy(sums.at[part], both_ref.at[part], sems.at[n])
        )
        copies[n].start()
    for copy in copies:
        copy.wait()


def near(x):
    return pltpu.with_memory_space_constraint(x, pltpu.VMEM)


FAR, NEAR = pltpu.HBM, pltpu.VMEM


def call(kernel, name, outs, weights, ins, bands=4, scalars=()):
    count, layers, rows, width = weights.shape
    return pl.pallas_call(
        kernel,
        in_specs=[pl.BlockSpec(memory_space=pltpu.SMEM)] * len(scalars)
        + [pl.BlockSpec(memory_space=pl.ANY)]
        + [VMEM] * len(ins),
        out_specs=[VMEM] * len(outs),
        out_shape=outs,
        scratch_shapes=[
            pltpu.VMEM((layers, count, rows, width), weights.dtype),
            pltpu.SemaphoreType.DMA((layers, bands)),
        ],
        compiler_params=SMALL,
        name=name,
    )(*scalars, pltpu.with_memory_space_constraint(weights, pltpu.HBM), *map(near, ins))


def local(inputs, guess_fwd, guess_adj, weights, biases, gains, cotangent):
    full_weights = lax.all_gather(weights, ("z", "c"))
    _, layers, _, width = full_weights.shape
    count = lax.axis_size("layer")
    index = lax.axis_index("layer")
    rows = inputs.shape[0]
    own = rows // count
    guess = guess_fwd[0]
    lam = guess_adj[0]
    arrived = from_behind(guess, "layer", 1)
    arrived_adj = from_behind(lam, "layer", -1)
    gains_all = lax.all_to_all(
        jnp.broadcast_to(gains[None], (count, 1, width)), "layer", 0, 0
    ).reshape(count, width)
    by_block = (count, own, width)
    guess_rows = lax.all_to_all(guess.reshape(by_block), "layer", 0, 0)
    lam_rows = lax.all_to_all(lam.reshape(by_block), "layer", 0, 0)
    anchor_rows = lax.dynamic_slice_in_dim(inputs, own * index, own)
    final_rows = lax.dynamic_slice_in_dim(cotangent, own * index, own)
    guess_start = jnp.where(index == 0, inputs.astype(f32), arrived)
    guess_end = jnp.where(index == count - 1, cotangent.astype(f32), arrived_adj)
    held = (guess_start, guess_end, gains_all, guess_rows, lam_rows)
    guess_start, guess_end, gains_all, guess_rows, lam_rows, anchor_rows, final_rows = (
        lax.optimization_barrier((*held, anchor_rows, final_rows))
    )
    tall = (rows, width)
    relaxed, relaxed_low = call(
        relax_kernel, "relax", [FAR(tall, f32), NEAR(tall, bf16)],
        full_weights, (guess_start, biases),
    )
    start = corrected(relaxed_low, guess_rows, gains_all, anchor_rows, False)
    every, later = (layers, rows, width), (layers - 1, rows, width)
    end_state, kept, slopes, back, back_low = call(
        both_ways_kernel, "both_ways",
        [FAR(tall, f32), NEAR(later, bf16), NEAR(every, f32), FAR(tall, f32), NEAR(tall, bf16)],
        full_weights, (start, biases, guess_end),
    )
    end_adj = corrected(back_low, lam_rows, gains_all, final_rows, True)
    core = lax.axis_index("c").astype(jnp.int32).reshape(1)
    chips, cores = lax.axis_size("z"), lax.axis_size("c")
    half = (chips, layers, width // (chips * cores), width)
    mine, theirs, adjoint, scaled = call(
        grads_kernel, "grads",
        [NEAR(half, bf16), NEAR(half, bf16), FAR(tall, f32), FAR(tall, bf16)],
        full_weights, (end_adj, slopes, start, kept), scalars=(core,),
    )
    theirs = lax.ppermute(theirs, "c", [(0, 1), (1, 0)])
    both = pl.pallas_call(
        add_kernel,
        in_specs=[VMEM] * 2,
        out_specs=pl.BlockSpec(memory_space=pl.ANY),
        out_shape=jax.ShapeDtypeStruct(half, bf16),
        scratch_shapes=[pltpu.VMEM(half, bf16), pltpu.SemaphoreType.DMA((4,))],
        compiler_params=SMALL,
        name="add_halves",
    )(near(mine), near(theirs))
    total = lax.psum_scatter(both, "z", scatter_dimension=0, tiled=True)
    adjoint = adjoint + back_step(scaled, square(full_weights[:, 0]))
    coarse = relaxed + gains * (start.astype(f32) - guess_start)
    coarse_adj = back + gains * (end_adj.astype(f32) - guess_end)
    return (
        end_state[None],
        adjoint[None],
        total[0].astype(f32),
        coarse[None],
        coarse_adj[None],
    )


def solution(mesh):
    layers, dp = mesh.devices.shape
    split = Mesh(mesh.devices.reshape(layers, dp // 2, 2), ("layer", "z", "c"))
    rows = ("z", "c")
    return jax.shard_map(
        local,
        mesh=split,
        in_specs=(
            P(rows, None),
            P("layer", rows, None),
            P("layer", rows, None),
            P("layer", rows, None),
            P("layer", None),
            P("layer", None),
            P(rows, None),
        ),
        out_specs=(
            P("layer", rows, None),
            P("layer", rows, None),
            P("layer", rows, None),
            P("layer", rows, None),
            P("layer", rows, None),
        ),
        check_vma=False,
    )
```

```python
import functools

import jax
import jax.numpy as jnp
from jax import lax
from jax.experimental import pallas as pl
from jax.experimental.pallas import tpu as pltpu
from jax.sharding import Mesh, PartitionSpec as P

step_size = 0.5
bf16 = jnp.bfloat16
f32 = jnp.float32
VMEM = pl.BlockSpec(memory_space=pltpu.VMEM)
SMALL = pltpu.CompilerParams(vmem_limit_bytes=20 * 2**20)


def from_behind(block, axis, distance):
    devices = range(lax.axis_size(axis))
    route = [(i - distance, i) for i in devices if i - distance in devices]
    return lax.ppermute(block, axis, route)


def scan_kernel(ends_ref, guess_ref, gains_ref, edge_ref, starts_ref, *, reverse):
    blocks = ends_ref.shape[0]
    carry = jnp.zeros(ends_ref.shape[1:], f32)
    order = range(blocks - 1, -1, -1) if reverse else range(blocks)
    step = -1 if reverse else 1
    starts_ref[order[0]] = edge_ref[...]
    for k in order[:-1]:
        guess = guess_ref[k]
        resid = ends_ref[k].astype(f32) - guess
        carry = gains_ref[k : k + 1, :] * carry + resid
        starts_ref[k + step] = (guess + carry).astype(starts_ref.dtype)


def corrected(end, guess_rows, gains_all, edge_rows, reverse):
    blocks = lax.axis_size("layer")
    rows, width = end.shape
    pieces = end.reshape(blocks, rows // blocks, width)
    mine = lax.all_to_all(pieces, "layer", 0, 0)
    starts = pl.pallas_call(
        functools.partial(scan_kernel, reverse=reverse),
        in_specs=[VMEM] * 4,
        out_specs=VMEM,
        out_shape=pltpu.VMEM(mine.shape, bf16),
        compiler_params=SMALL,
        name="coarse_scan",
    )(*map(near, (mine, guess_rows, gains_all, edge_rows)))
    return lax.all_to_all(starts, "layer", 0, 0).reshape(rows, width)


def fetch(weights_hbm, held, sems, layers):
    bands = sems.shape[1]
    size = held.shape[1] // bands
    copies = {}
    for l in layers:
        for n in range(bands):
            band = pl.ds(n * size, size)
            copies[l, n] = pltpu.make_async_copy(
                weights_hbm.at[band, l], held.at[l, band], sems.at[l, n]
            )
            copies[l, n].start()
    return copies


def forward_layer(rounded, l, held, biases_ref, copies, bands):
    size = held.shape[1] // bands
    width = held.shape[3]
    total = biases_ref[l : l + 1, :]
    for n in range(bands):
        copies[l, n].wait()
        weight = held[l, n * size : (n + 1) * size].reshape(-1, width)
        tall = weight.shape[0]
        total = total + jnp.dot(
            rounded[:, n * tall : (n + 1) * tall], weight, preferred_element_type=f32
        )
    return jnp.tanh(total)


def square(weight):
    return weight.reshape(-1, weight.shape[-1])


def back_step(scaled, weight):
    return step_size * lax.dot_general(
        scaled, weight, (((1,), (1,)), ((), ())), preferred_element_type=f32
    )


def relax_kernel(w_ref, start_ref, b_ref, end_ref, rounded_ref, held, sems):
    layers, bands = sems.shape
    copies = fetch(w_ref, held, sems, range(layers))
    state = start_ref[...]
    for l in range(layers):
        active = forward_layer(state.astype(bf16), l, held, b_ref, copies, bands)
        state = state + step_size * active
    end_ref[...] = state
    rounded_ref[...] = state.astype(bf16)


def both_ways_kernel(
    w_ref, start_ref, b_ref, adj_ref,
    end_ref, kept_ref, slopes_ref, back_ref, rounded_ref, held, sems,
):
    layers, bands = sems.shape
    copies = fetch(w_ref, held, sems, range(layers))
    state = start_ref[...].astype(f32)
    for l in range(layers):
        rounded = state.astype(bf16)
        if l:
            kept_ref[l - 1] = rounded
        active = forward_layer(rounded, l, held, b_ref, copies, bands)
        slopes_ref[l] = 1.0 - active * active
        state = state + step_size * active
    end_ref[...] = state
    adjoint = adj_ref[...]
    for l in reversed(range(layers)):
        scaled = (adjoint * slopes_ref[l]).astype(bf16)
        adjoint = adjoint + back_step(scaled, square(held[l]))
    back_ref[...] = adjoint
    rounded_ref[...] = adjoint.astype(bf16)


def scaled_kernel(
    w_ref, adj_ref, slopes_ref, start_ref, kept_ref, send_ref, held, sems
):
    layers, bands = sems.shape
    copies = fetch(w_ref, held, sems, range(layers - 1, 0, -1))
    send_ref[0] = start_ref[...]
    for l in range(1, layers):
        send_ref[l] = kept_ref[l - 1]
    adjoint = adj_ref[...].astype(f32)
    send_ref[2 * layers - 1] = (adjoint * slopes_ref[layers - 1]).astype(bf16)
    size = held.shape[1] // bands
    for l in range(layers - 1, 0, -1):
        scaled = send_ref[layers + l]
        parts = []
        for n in range(bands):
            copies[l, n].wait()
            weight = square(held[l, n * size : (n + 1) * size])
            tall = weight.shape[0]
            at = slice(n * tall, (n + 1) * tall)
            parts.append(adjoint[:, at] + back_step(scaled, weight))
            send_ref[layers + l - 1, :, at] = (
                parts[n] * slopes_ref[l - 1, :, at]
            ).astype(bf16)
        if l > 1:
            adjoint = jnp.concatenate(parts, 1)


def grads_kernel(core_ref, mine_ref, theirs_ref, both_ref, picked, sums, sems):
    layers = sums.shape[1]
    chips, _, rows, width = sums.shape
    first = core_ref[0] == 0
    deep = mine_ref.shape[1]
    copies = []
    for l in range(layers):
        for at, ref in ((0, mine_ref), (deep, theirs_ref)):
            turned = ref[l].T.reshape(chips, 2, rows, deep)
            picked[:, at : at + deep] = square(
                jnp.where(first, turned[:, 0], turned[:, 1])
            )
        scaled = jnp.concatenate([mine_ref[layers + l], theirs_ref[layers + l]], 0)
        grad = step_size * jnp.dot(picked[...], scaled, preferred_element_type=f32)
        sums[:, l] = grad.reshape(chips, rows, width).astype(bf16)
        copies.append(
            pltpu.make_async_copy(sums.at[:, l], both_ref.at[:, l], sems.at[l])
        )
        copies[l].start()
    for copy in copies:
        copy.wait()


def near(x):
    return pltpu.with_memory_space_constraint(x, pltpu.VMEM)


FAR, NEAR = pltpu.HBM, pltpu.VMEM


def call(kernel, name, outs, weights, ins, bands=4):
    count, layers, rows, width = weights.shape
    return pl.pallas_call(
        kernel,
        in_specs=[pl.BlockSpec(memory_space=pl.ANY)] + [VMEM] * len(ins),
        out_specs=[VMEM] * len(outs),
        out_shape=outs,
        scratch_shapes=[
            pltpu.VMEM((layers, count, rows, width), weights.dtype),
            pltpu.SemaphoreType.DMA((layers, bands)),
        ],
        compiler_params=SMALL,
        name=name,
    )(pltpu.with_memory_space_constraint(weights, pltpu.HBM), *map(near, ins))


def local(inputs, guess_fwd, guess_adj, weights, biases, gains, cotangent):
    full_weights = lax.all_gather(weights, ("z", "c"))
    _, layers, _, width = full_weights.shape
    count = lax.axis_size("layer")
    index = lax.axis_index("layer")
    rows = inputs.shape[0]
    own = rows // count
    guess = guess_fwd[0]
    lam = guess_adj[0]
    arrived = from_behind(guess, "layer", 1)
    arrived_adj = from_behind(lam, "layer", -1)
    gains_all = lax.all_to_all(
        jnp.broadcast_to(gains[None], (count, 1, width)), "layer", 0, 0
    ).reshape(count, width)
    by_block = (count, own, width)
    guess_rows = lax.all_to_all(guess.reshape(by_block), "layer", 0, 0)
    lam_rows = lax.all_to_all(lam.reshape(by_block), "layer", 0, 0)
    anchor_rows = lax.dynamic_slice_in_dim(inputs, own * index, own)
    final_rows = lax.dynamic_slice_in_dim(cotangent, own * index, own)
    guess_start = jnp.where(index == 0, inputs.astype(f32), arrived)
    guess_end = jnp.where(index == count - 1, cotangent.astype(f32), arrived_adj)
    held = (guess_start, guess_end, gains_all, guess_rows, lam_rows)
    guess_start, guess_end, gains_all, guess_rows, lam_rows, anchor_rows, final_rows = (
        lax.optimization_barrier((*held, anchor_rows, final_rows))
    )
    tall = (rows, width)
    relaxed, relaxed_low = call(
        relax_kernel, "relax", [FAR(tall, f32), NEAR(tall, bf16)],
        full_weights, (guess_start, biases),
    )
    start = corrected(relaxed_low, guess_rows, gains_all, anchor_rows, False)
    every, later = (layers, rows, width), (layers - 1, rows, width)
    end_state, kept, slopes, back, back_low = call(
        both_ways_kernel, "both_ways",
        [FAR(tall, f32), NEAR(later, bf16), NEAR(every, f32), FAR(tall, f32), NEAR(tall, bf16)],
        full_weights, (start, biases, guess_end),
    )
    end_adj = corrected(back_low, lam_rows, gains_all, final_rows, True)
    core = lax.axis_index("c").astype(jnp.int32).reshape(1)
    chips, cores = lax.axis_size("z"), lax.axis_size("c")
    part = (chips, layers, width // (chips * cores), width)
    (mine,) = call(
        scaled_kernel, "scaled", [NEAR((2 * layers, rows, width), bf16)],
        full_weights, (end_adj, slopes, start, kept),
    )
    theirs = lax.ppermute(mine, "c", [(0, 1), (1, 0)])
    both = pl.pallas_call(
        grads_kernel,
        in_specs=[pl.BlockSpec(memory_space=pltpu.SMEM), VMEM, VMEM],
        out_specs=pl.BlockSpec(memory_space=pl.ANY),
        out_shape=FAR(part, bf16),
        scratch_shapes=[
            pltpu.VMEM((width // cores, cores * rows), bf16),
            pltpu.VMEM(part, bf16),
            pltpu.SemaphoreType.DMA((layers,)),
        ],
        compiler_params=SMALL,
        name="grads",
    )(core, near(mine), near(theirs))
    total = lax.psum_scatter(both, "z", scatter_dimension=0, tiled=True)
    adjoint = end_adj.astype(f32)
    for l in reversed(range(layers)):
        adjoint = adjoint + back_step(mine[layers + l], square(full_weights[:, l]))
    coarse = relaxed + gains * (start.astype(f32) - guess_start)
    coarse_adj = back + gains * (end_adj.astype(f32) - guess_end)
    return (
        end_state[None],
        adjoint[None],
        total[0].astype(f32),
        coarse[None],
        coarse_adj[None],
    )


def solution(mesh):
    layers, dp = mesh.devices.shape
    split = Mesh(mesh.devices.reshape(layers, dp // 2, 2), ("layer", "z", "c"))
    rows = ("z", "c")
    return jax.shard_map(
        local,
        mesh=split,
        in_specs=(
            P(rows, None),
            P("layer", rows, None),
            P("layer", rows, None),
            P("layer", rows, None),
            P("layer", None),
            P("layer", None),
            P(rows, None),
        ),
        out_specs=(
            P("layer", rows, None),
            P("layer", rows, None),
            P("layer", rows, None),
            P("layer", rows, None),
            P("layer", rows, None),
        ),
        check_vma=False,
    )
```

```python
import functools

import jax
import jax.numpy as jnp
from jax import lax
from jax.experimental import pallas as pl
from jax.experimental.pallas import tpu as pltpu
from jax.sharding import Mesh, PartitionSpec as P

step_size = 0.5
bf16 = jnp.bfloat16
f32 = jnp.float32
VMEM = pl.BlockSpec(memory_space=pltpu.VMEM)
SMALL = pltpu.CompilerParams(vmem_limit_bytes=20 * 2**20)


def from_behind(block, axis, distance):
    devices = range(lax.axis_size(axis))
    route = [(i - distance, i) for i in devices if i - distance in devices]
    return lax.ppermute(block, axis, route)


def scan_kernel(ends_ref, guess_ref, gains_ref, edge_ref, starts_ref, *, reverse):
    blocks = ends_ref.shape[0]
    carry = jnp.zeros(ends_ref.shape[1:], f32)
    order = range(blocks - 1, -1, -1) if reverse else range(blocks)
    step = -1 if reverse else 1
    starts_ref[order[0]] = edge_ref[...]
    for k in order[:-1]:
        guess = guess_ref[k]
        resid = ends_ref[k].astype(f32) - guess
        carry = gains_ref[k : k + 1, :] * carry + resid
        starts_ref[k + step] = (guess + carry).astype(starts_ref.dtype)


def corrected(end, guess_rows, gains_all, edge_rows, reverse):
    blocks = lax.axis_size("layer")
    rows, width = end.shape
    pieces = end.reshape(blocks, rows // blocks, width)
    mine = lax.all_to_all(pieces, "layer", 0, 0)
    starts = pl.pallas_call(
        functools.partial(scan_kernel, reverse=reverse),
        in_specs=[VMEM] * 4,
        out_specs=VMEM,
        out_shape=pltpu.VMEM(mine.shape, bf16),
        compiler_params=SMALL,
        name="coarse_scan",
    )(*map(near, (mine, guess_rows, gains_all, edge_rows)))
    return lax.all_to_all(starts, "layer", 0, 0).reshape(rows, width)


def fetch(weights_hbm, held, sems, layers):
    bands = sems.shape[1]
    size = held.shape[1] // bands
    copies = {}
    for l in layers:
        for n in range(bands):
            band = pl.ds(n * size, size)
            copies[l, n] = pltpu.make_async_copy(
                weights_hbm.at[band, l], held.at[l, band], sems.at[l, n]
            )
            copies[l, n].start()
    return copies


def forward_layer(rounded, l, held, biases_ref, copies, bands):
    size = held.shape[1] // bands
    width = held.shape[3]
    total = biases_ref[l : l + 1, :]
    for n in range(bands):
        copies[l, n].wait()
        weight = held[l, n * size : (n + 1) * size].reshape(-1, width)
        tall = weight.shape[0]
        total = total + jnp.dot(
            rounded[:, n * tall : (n + 1) * tall], weight, preferred_element_type=f32
        )
    return jnp.tanh(total)


def square(weight):
    return weight.reshape(-1, weight.shape[-1])


def back_step(scaled, weight):
    return step_size * lax.dot_general(
        scaled, weight, (((1,), (1,)), ((), ())), preferred_element_type=f32
    )


def relax_kernel(w_ref, start_ref, b_ref, end_ref, rounded_ref, held, sems):
    layers, bands = sems.shape
    copies = fetch(w_ref, held, sems, range(layers))
    state = start_ref[...]
    for l in range(layers):
        active = forward_layer(state.astype(bf16), l, held, b_ref, copies, bands)
        state = state + step_size * active
    end_ref[...] = state
    rounded_ref[...] = state.astype(bf16)


def both_ways_kernel(
    w_ref, start_ref, b_ref, adj_ref,
    end_ref, kept_ref, slopes_ref, back_ref, rounded_ref, held, sems,
):
    layers, bands = sems.shape
    copies = fetch(w_ref, held, sems, range(layers))
    state = start_ref[...].astype(f32)
    for l in range(layers):
        rounded = state.astype(bf16)
        if l:
            kept_ref[l - 1] = rounded
        active = forward_layer(rounded, l, held, b_ref, copies, bands)
        slopes_ref[l] = 1.0 - active * active
        state = state + step_size * active
    end_ref[...] = state
    adjoint = adj_ref[...]
    for l in reversed(range(layers)):
        scaled = (adjoint * slopes_ref[l]).astype(bf16)
        adjoint = adjoint + back_step(scaled, square(held[l]))
    back_ref[...] = adjoint
    rounded_ref[...] = adjoint.astype(bf16)


def scaled_kernel(
    w_ref, adj_ref, slopes_ref, start_ref, kept_ref, send_ref, held, sems
):
    layers, bands = sems.shape
    copies = fetch(w_ref, held, sems, range(layers - 1, 0, -1))
    send_ref[0] = start_ref[...]
    for l in range(1, layers):
        send_ref[l] = kept_ref[l - 1]
    adjoint = adj_ref[...].astype(f32)
    send_ref[2 * layers - 1] = (adjoint * slopes_ref[layers - 1]).astype(bf16)
    size = held.shape[1] // bands
    for l in range(layers - 1, 0, -1):
        scaled = send_ref[layers + l]
        parts = []
        for n in range(bands):
            copies[l, n].wait()
            weight = square(held[l, n * size : (n + 1) * size])
            tall = weight.shape[0]
            at = slice(n * tall, (n + 1) * tall)
            parts.append(adjoint[:, at] + back_step(scaled, weight))
            send_ref[layers + l - 1, :, at] = (
                parts[n] * slopes_ref[l - 1, :, at]
            ).astype(bf16)
        if l > 1:
            adjoint = jnp.concatenate(parts, 1)


def grads_kernel(
    core_ref, mine_ref, theirs_hbm, both_ref, picked, sums, sems, theirs_ref, arrived
):
    layers = sums.shape[1]
    chips, _, rows, width = sums.shape
    first = core_ref[0] == 0
    deep = mine_ref.shape[1]
    copies = []
    coming = [
        pltpu.make_async_copy(theirs_hbm.at[i], theirs_ref.at[i], arrived.at[i])
        for i in range(2 * layers)
    ]
    for l in range(layers):
        coming[l].start()
        coming[layers + l].start()
    for l in range(layers):
        for at, ref in ((0, mine_ref), (deep, theirs_ref)):
            if at:
                coming[l].wait()
            turned = ref[l].T.reshape(chips, 2, rows, deep)
            picked[:, at : at + deep] = square(
                jnp.where(first, turned[:, 0], turned[:, 1])
            )
        coming[layers + l].wait()
        scaled = jnp.concatenate([mine_ref[layers + l], theirs_ref[layers + l]], 0)
        grad = step_size * jnp.dot(picked[...], scaled, preferred_element_type=f32)
        sums[:, l] = grad.reshape(chips, rows, width).astype(bf16)
        copies.append(
            pltpu.make_async_copy(sums.at[:, l], both_ref.at[:, l], sems.at[l])
        )
        copies[l].start()
    for copy in copies:
        copy.wait()


def near(x):
    return pltpu.with_memory_space_constraint(x, pltpu.VMEM)


FAR, NEAR = pltpu.HBM, pltpu.VMEM


def call(kernel, name, outs, weights, ins, bands=4):
    count, layers, rows, width = weights.shape
    return pl.pallas_call(
        kernel,
        in_specs=[pl.BlockSpec(memory_space=pl.ANY)] + [VMEM] * len(ins),
        out_specs=[VMEM] * len(outs),
        out_shape=outs,
        scratch_shapes=[
            pltpu.VMEM((layers, count, rows, width), weights.dtype),
            pltpu.SemaphoreType.DMA((layers, bands)),
        ],
        compiler_params=SMALL,
        name=name,
    )(pltpu.with_memory_space_constraint(weights, pltpu.HBM), *map(near, ins))


def local(inputs, guess_fwd, guess_adj, weights, biases, gains, cotangent):
    full_weights = lax.all_gather(weights, ("z", "c"))
    _, layers, _, width = full_weights.shape
    count = lax.axis_size("layer")
    index = lax.axis_index("layer")
    rows = inputs.shape[0]
    own = rows // count
    guess = guess_fwd[0]
    lam = guess_adj[0]
    arrived = from_behind(guess, "layer", 1)
    arrived_adj = from_behind(lam, "layer", -1)
    gains_all = lax.all_to_all(
        jnp.broadcast_to(gains[None], (count, 1, width)), "layer", 0, 0
    ).reshape(count, width)
    by_block = (count, own, width)
    guess_rows = lax.all_to_all(guess.reshape(by_block), "layer", 0, 0)
    lam_rows = lax.all_to_all(lam.reshape(by_block), "layer", 0, 0)
    anchor_rows = lax.dynamic_slice_in_dim(inputs, own * index, own)
    final_rows = lax.dynamic_slice_in_dim(cotangent, own * index, own)
    guess_start = jnp.where(index == 0, inputs.astype(f32), arrived)
    guess_end = jnp.where(index == count - 1, cotangent.astype(f32), arrived_adj)
    held = (guess_start, guess_end, gains_all, guess_rows, lam_rows)
    guess_start, guess_end, gains_all, guess_rows, lam_rows, anchor_rows, final_rows = (
        lax.optimization_barrier((*held, anchor_rows, final_rows))
    )
    tall = (rows, width)
    relaxed, relaxed_low = call(
        relax_kernel, "relax", [FAR(tall, f32), NEAR(tall, bf16)],
        full_weights, (guess_start, biases),
    )
    start = corrected(relaxed_low, guess_rows, gains_all, anchor_rows, False)
    every, later = (layers, rows, width), (layers - 1, rows, width)
    end_state, kept, slopes, back, back_low = call(
        both_ways_kernel, "both_ways",
        [FAR(tall, f32), NEAR(later, bf16), NEAR(every, f32), FAR(tall, f32), NEAR(tall, bf16)],
        full_weights, (start, biases, guess_end),
    )
    end_adj = corrected(back_low, lam_rows, gains_all, final_rows, True)
    core = lax.axis_index("c").astype(jnp.int32).reshape(1)
    chips, cores = lax.axis_size("z"), lax.axis_size("c")
    part = (chips, layers, width // (chips * cores), width)
    (mine,) = call(
        scaled_kernel, "scaled", [NEAR((2 * layers, rows, width), bf16)],
        full_weights, (end_adj, slopes, start, kept),
    )
    theirs = lax.ppermute(mine, "c", [(0, 1), (1, 0)])
    both = pl.pallas_call(
        grads_kernel,
        in_specs=[
            pl.BlockSpec(memory_space=pltpu.SMEM),
            VMEM,
            pl.BlockSpec(memory_space=pl.ANY),
        ],
        out_specs=pl.BlockSpec(memory_space=pl.ANY),
        out_shape=FAR(part, bf16),
        scratch_shapes=[
            pltpu.VMEM((width // cores, cores * rows), bf16),
            pltpu.VMEM(part, bf16),
            pltpu.SemaphoreType.DMA((layers,)),
            pltpu.VMEM(mine.shape, bf16),
            pltpu.SemaphoreType.DMA((2 * layers,)),
        ],
        compiler_params=SMALL,
        name="grads",
    )(core, near(mine), theirs)
    total = lax.psum_scatter(both, "z", scatter_dimension=0, tiled=True)
    adjoint = end_adj.astype(f32)
    for l in reversed(range(layers)):
        adjoint = adjoint + back_step(mine[layers + l], square(full_weights[:, l]))
    coarse = relaxed + gains * (start.astype(f32) - guess_start)
    coarse_adj = back + gains * (end_adj.astype(f32) - guess_end)
    return (
        end_state[None],
        adjoint[None],
        total[0].astype(f32),
        coarse[None],
        coarse_adj[None],
    )


def solution(mesh):
    layers, dp = mesh.devices.shape
    split = Mesh(mesh.devices.reshape(layers, dp // 2, 2), ("layer", "z", "c"))
    rows = ("z", "c")
    return jax.shard_map(
        local,
        mesh=split,
        in_specs=(
            P(rows, None),
            P("layer", rows, None),
            P("layer", rows, None),
            P("layer", rows, None),
            P("layer", None),
            P("layer", None),
            P(rows, None),
        ),
        out_specs=(
            P("layer", rows, None),
            P("layer", rows, None),
            P("layer", rows, None),
            P("layer", rows, None),
            P("layer", rows, None),
        ),
        check_vma=False,
    )
```
